32 devices in a mesh: dp: 8 (over y, x, core), tensor: 4 (over z).
Axes of the slice: x: 2, y: 2, z: 4, core: 2. Of those that a mesh axis runs over, the one named last changes fastest.
Arguments:
- activations: bfloat16 [8192, 2048], P(('dp', 'tensor')), may hold values from -12 to 12
- sequence_start: int32 [8192], P(('dp', 'tensor')), may hold values from 0 to 512, as said below
- norm_gain: bfloat16 [2, 2048], P(None, ('dp', 'tensor')), may hold values from 0.25 to 1.75
- norm_bias: bfloat16 [2, 2048], P(None, ('dp', 'tensor')), may hold values from -1.75 to 1.75
- projection: bfloat16 [2048, 3, 2048], P('dp', None, 'tensor'), may hold values from -2 to 2
- biases: bfloat16 [2, 32, 64], P(None, 'tensor', 'dp'), may hold values from -3 to 3
- rotary_bias: bfloat16 [32, 16], P('tensor', 'dp'), may hold values from -6 to 6
- merge_weight: bfloat16 [2048, 2048], P('tensor', 'dp'), may hold values from -0.5 to 0.5
- expand_weight: bfloat16 [2048, 2, 5632], P('dp', None, 'tensor'), may hold values from -0.125 to 0.125
- down_weight: bfloat16 [5632, 2048], P('tensor', 'dp'), may hold values from -0.078125 to 0.078125
- cotangent: bfloat16 [8192, 2048], P(('dp', 'tensor')), may hold values from -12 to 12
Outputs:
- layer_output: bfloat16 [8192, 2048], P(('dp', 'tensor'))
- input_grad: float32 [8192, 2048], P(('dp', 'tensor'))
- gain_grad: float32 [2, 2048], P(None, ('dp', 'tensor'))
- shift_grad: float32 [2, 2048], P(None, ('dp', 'tensor'))
- projection_grad: float32 [2048, 3, 2048], P('dp', None, 'tensor')
- biases_grad: float32 [2, 32, 64], P(None, 'tensor', 'dp')
- rotary_grad: float32 [32, 16], P('tensor', 'dp')
- merge_grad: float32 [2048, 2048], P('tensor', 'dp')
- expand_grad: float32 [2048, 2, 5632], P('dp', None, 'tensor')
- down_grad: float32 [5632, 2048], P('tensor', 'dp')
The draws below stay inside these ranges and needn't reach their ends.
Inputs may be any that keep to these rules, and one draw needn't show every extreme that they name: `sequence_start`: each sequence lies within one data group of 1024 tokens and starts at a multiple of 512; sequences have 512 to 1024 tokens; group 0 holds a single sequence and the last group only sequences of 512 tokens.
All inputs are finite; a program needn't handle non-finite values.
Results may differ from the reference program's by a relative error of at most 0.03.
Values may be sent and summed in bfloat16 or wider, within the bound.
No kernel may reach another device: no remote copies, remote signals or barrier semaphores. Data moves between devices by JAX's collectives and lax.ppermute only.
A program may use at most 192 MiB of HBM per device.

```python
import math
from functools import partial
import jax
import jax.numpy as jnp
from jax import lax

D = 2048
H = 32
HD = 64
ROT = 16
FF = 5632
MIN_LEN = 512
GROUP = 1024
TOKENS = 8192
N_TENSOR = 4


def draw_sequence_start(key, part):
    groups = TOKENS // GROUP
    blocks = GROUP // MIN_LEN
    coin_flips = jax.random.randint(key, (groups, blocks), 0, 2)
    group_index = jnp.arange(groups, dtype=jnp.int32)[:, None]
    block_index = jnp.arange(blocks, dtype=jnp.int32)[None, :]
    boundary = jnp.where(group_index == 0, 0, jnp.where(group_index == groups - 1, 1, coin_flips))
    boundary = jnp.where(block_index == 0, 1, boundary)
    starts = lax.cummax(boundary * block_index * MIN_LEN, axis=1)
    return jnp.repeat(starts, MIN_LEN, axis=1).reshape(TOKENS).astype(jnp.int32)


def draw_projection(key, part):
    normal_part = jax.random.normal(key, (D, 3, D), jnp.float32) / math.sqrt(D)
    return jnp.clip(normal_part, -2.0, 2.0).astype(jnp.bfloat16)


def raised(entries, own_key, source, target, parts, factor):
    owner, partner = [(jnp.arange(entries.shape[position]) // (entries.shape[position] // parts)).reshape([-1 if axis == position else 1 for axis in range(entries.ndim)]) for position in (source, target)]
    chosen = jax.random.permutation(own_key, parts)[partner]
    strong = (owner == chosen) | (owner == (partner + parts // 2) % parts)
    return jnp.where(strong, factor * entries, entries)


def shard_levels(key, dims, cuts, smallest, largest):
    def one(axis_at, blocks):
        steps = jax.random.uniform(jax.random.fold_in(jax.random.fold_in(key, 6), axis_at), (blocks,), jnp.float32, smallest / len(cuts), largest / len(cuts))
        return jnp.repeat(jnp.exp(steps), dims[axis_at] // blocks).reshape((-1,) + (1,) * (len(dims) - axis_at - 1))

    factor_of = one(*cuts[0])
    for cut in cuts[1:]:
        factor_of = factor_of * one(*cut)
    return factor_of


def noise(key, dims, spread, limit, cuts=(), kind=jnp.bfloat16):
    level = shard_levels(key, dims, cuts, -0.22, 0.18) if cuts else 1.0
    values = jax.random.normal(key, dims, jnp.float32) * spread * level
    return jnp.minimum(jnp.maximum(values, -limit), limit).astype(kind)


def bell_draw_with(stream_key, dims, deviation, reach, cuts, heavy, held_as=jnp.bfloat16):
    entries = deviation * jax.random.normal(stream_key, dims, jnp.float32)
    if cuts:
        entries = entries * shard_levels(stream_key, dims, cuts, -0.22, 0.18)
    return jnp.clip(raised(entries, jax.random.fold_in(stream_key, 3), *heavy), -reach, reach).astype(held_as)


def setup_inputs(seed: int = 0) -> dict:
    splits = jax.random.split(jax.random.key(seed), 12)
    return {
        "activations": bell_draw_with(splits[0], (TOKENS, D), 1.0, 12.0, ((0, 32),), (0, 1, 32, 2.75)),
        "sequence_start": draw_sequence_start(jax.random.fold_in(splits[11], 71), 0),
        "norm_gain": jnp.clip(1.0 + 0.15 * jax.random.normal(splits[2], (2, D), jnp.float32), 0.25, 1.75).astype(jnp.bfloat16),
        "norm_bias": noise(splits[3], (2, D), 0.3, 1.75, ((1, 32),)),
        "projection": draw_projection(jax.random.fold_in(splits[11], 71), 0),
        "biases": noise(splits[5], (2, H, HD), 0.5, 3.0, ((1, 4), (2, 8))),
        "rotary_bias": noise(splits[6], (H, ROT), 1.0, 6.0, ((0, 4), (1, 8))),
        "merge_weight": noise(splits[7], (D, D), (D // 16) ** -0.5, 0.5, ((0, 4), (1, 8))),
        "expand_weight": noise(splits[8], (D, 2, FF), D ** -0.5, 0.125, ((0, 8), (2, 4))),
        "down_weight": noise(splits[9], (FF, D), FF ** -0.5, 0.078125, ((0, 4), (1, 8))),
        "cotangent": bell_draw_with(splits[10], (TOKENS, D), 1.0, 12.0, ((0, 32),), (0, 1, 32, 2.75)),
    }


@jax.custom_vjp
def low(v):
    return lax.optimization_barrier(v.astype(jnp.bfloat16)).astype(jnp.float32)

@jax.custom_vjp
def low_back(v):
    return v

def low_keep(v):
    return (low(v), None)

def low_pass(kept, grad):
    return (grad,)

def back_keep(v):
    return (v, None)

def back_low(kept, grad):
    return (low(grad),)
low.defvjp(low_keep, low_pass)
low_back.defvjp(back_keep, back_low)
EPSILON = 1e-05
NEGATIVE = -1e+30
ROPE_BASE = 10000.0
HIGHEST = lax.Precision.HIGHEST

def layer_norm(values, scales, shifts):
    centred = values - lax.optimization_barrier(jnp.mean(values, axis=-1, keepdims=True))
    variance = lax.optimization_barrier(jnp.mean(centred * centred, axis=-1, keepdims=True))
    return centred * lax.rsqrt(variance + EPSILON) * scales + shifts

def rotary(values, angles):
    half_rot = angles.shape[-1]
    cosine = jnp.cos(angles)[:, None, :]
    sine_part = jnp.sin(angles)[:, None, :]
    first_half = values[..., :half_rot]
    second_half = values[..., half_rot:2 * half_rot]
    return jnp.concatenate([first_half * cosine - second_half * sine_part, second_half * cosine + first_half * sine_part, values[..., 2 * half_rot:]], axis=-1)

def rope_angles(positions):
    inverse = jnp.power(ROPE_BASE, -2.0 * jnp.arange(ROT // 2, dtype=jnp.float32) / ROT)
    return positions.astype(jnp.float32)[:, None] * inverse[None, :]

def attend_group(operands):
    queries, keys_all, values, starts = operands
    length = queries.shape[0]
    block_rows = min(512, length)
    factor = 1.0 / math.sqrt(HD)
    places = jnp.arange(length, dtype=jnp.int32)

    def block_out(pieces):
        query_block, place_block, start_block = pieces
        scores = jnp.einsum('qhd,khd->hqk', query_block, keys_all, precision=HIGHEST) * factor
        scores = low_back(scores)
        allowed = (places[None, :] <= place_block[:, None]) & (starts[None, :] == start_block[:, None])
        scores = jnp.where(allowed[None], scores, NEGATIVE)
        row_peak = lax.optimization_barrier(jnp.max(scores, axis=-1, keepdims=True))
        weights = jnp.exp(scores - row_peak)
        shares = low(weights / lax.optimization_barrier(jnp.sum(weights, axis=-1, keepdims=True)))
        return jnp.einsum('hqk,khd->qhd', shares, values, precision=HIGHEST)
    blocks = length // block_rows
    result = lax.map(jax.checkpoint(block_out), (queries.reshape(blocks, block_rows, H, HD), places.reshape(blocks, block_rows), starts.reshape(blocks, block_rows)))
    return result.reshape(length, H, HD)

def forward(activations, norm_gain, norm_bias, projection, biases, rotary_bias, merge_weight, expand_weight, down_weight, starts):
    tokens = activations.shape[0]
    width_part = D // N_TENSOR
    hidden_part = FF // N_TENSOR
    normed = low(layer_norm(activations, norm_gain[0], norm_bias[0]))
    pieces = []
    for group in range(N_TENSOR):
        copied = low_back(normed)
        pieces.append(jnp.einsum('nd,dcf->ncf', copied, projection[:, :, group * width_part:(group + 1) * width_part], precision=HIGHEST))
    projected = jnp.concatenate(pieces, axis=2).reshape(tokens, 3, H, HD)
    key_shift = jnp.pad(rotary_bias, ((0, 0), (0, HD - ROT)))
    query_lin = projected[:, 0] + biases[0]
    key_lin = projected[:, 1] + key_shift
    value_lin = projected[:, 2] + biases[1]
    places = jnp.arange(tokens, dtype=jnp.int32) % GROUP
    angles = rope_angles(places - starts)
    queries = low(rotary(low_back(query_lin), angles))
    keys_all = low(rotary(low_back(key_lin), angles))
    values = low(low_back(value_lin))
    groups = tokens // GROUP
    group_shape = (groups, GROUP, H, HD)
    attended = lax.map(jax.checkpoint(attend_group), (queries.reshape(group_shape), keys_all.reshape(group_shape), values.reshape(group_shape), starts.reshape(groups, GROUP)))
    attended = low(low_back(attended.reshape(tokens, D)))
    branch = jnp.zeros((tokens, D), jnp.float32)
    for group in range(N_TENSOR):
        lower = group * width_part
        branch = branch + low(jnp.dot(attended[:, lower:lower + width_part], merge_weight[lower:lower + width_part], precision=HIGHEST, preferred_element_type=jnp.float32))
    branch = low_back(branch)
    residual = activations + branch
    normed_two = low(layer_norm(residual, norm_gain[1], norm_bias[1]))
    feed_out = jnp.zeros((tokens, D), jnp.float32)
    for group in range(N_TENSOR):
        lower = group * hidden_part
        copied = low_back(normed_two)
        expanded = jnp.einsum('nd,dcf->ncf', copied, expand_weight[:, :, lower:lower + hidden_part], precision=HIGHEST)
        gate_part = low_back(expanded[:, 0])
        up_part = low_back(expanded[:, 1])
        hidden = low(jax.nn.silu(gate_part) * up_part)
        feed_out = feed_out + low(jnp.dot(hidden, down_weight[lower:lower + hidden_part], precision=HIGHEST, preferred_element_type=jnp.float32))
    feed_out = low_back(feed_out)
    return residual + feed_out

def reference(activations, sequence_start, norm_gain, norm_bias, projection, biases, rotary_bias, merge_weight, expand_weight, down_weight, cotangent):
    floats = [array.astype(jnp.float32) for array in (activations, norm_gain, norm_bias, projection, biases, rotary_bias, merge_weight, expand_weight, down_weight)]
    output, pullback = jax.vjp(partial(forward, starts=sequence_start.astype(jnp.int32)), *floats)
    grads = pullback(cotangent.astype(jnp.float32))
    return (output.astype(jnp.bfloat16), grads[0], grads[1], grads[2], grads[3], grads[4], grads[5], grads[6], grads[7], grads[8])
```

```python
import math

import jax
import jax.numpy as jnp
from jax import lax
from jax.experimental import pallas as pl
from jax.experimental.pallas import tpu as pltpu
from jax.sharding import PartitionSpec as P

CHUNKS = 2
HD = 64
ROT = 16


EPSILON = 1e-05
NEGATIVE = -1e30
ROPE_BASE = 10000.0
ROWS = (((0,), (0,)), ((), ()))
COLS = (((1,), (1,)), ((), ()))
F32 = jnp.float32
BF16 = jnp.bfloat16


def norm_stats(values):
    mean = jnp.mean(values, axis=-1, keepdims=True)
    centred = values - mean
    variance = jnp.mean(centred * centred, axis=-1, keepdims=True)
    scale = lax.rsqrt(variance + EPSILON)
    return centred * scale, scale


def norm_back(unit, scale, gains, grads):
    w = grads * gains
    return (
        w - jnp.mean(w, axis=-1, keepdims=True) - unit * jnp.mean(w * unit, axis=-1, keepdims=True)
    ) * scale


NT = (((1,), (1,)), ((), ()))
NN = (((1,), (0,)), ((), ()))
TILE = 256
BLOCK = 512
PAIR = 128


def mx(a, b, dims):
    return lax.dot_general(a, b, dims, preferred_element_type=F32)


def head_lanes(rows, head):
    lane = lax.broadcasted_iota(jnp.int32, (rows, PAIR), 1)
    return lane < HD if head == 0 else lane >= HD


def attend_kernel(
    first_ref,
    q_lin,
    k_lin,
    v_lin,
    q_bias,
    k_bias,
    v_bias,
    cos_ref,
    low_ref,
    high_ref,
    q_out,
    k_out,
    v_out,
    o_out,
    log_out,
    scaled,
):
    rows = q_lin.shape[0]
    pair = pl.program_id(0)
    half = ROT // 2

    def turn(values, at):
        return (
            values * cos_ref[at, :]
            + pltpu.roll(values, PAIR - half, 1) * low_ref[at, :]
            + pltpu.roll(values, half, 1) * high_ref[at, :]
        )

    for start in range(0, rows, TILE):
        at = pl.ds(start, TILE)
        q = turn(q_lin[at, :] + q_bias[...], at).astype(BF16)
        q_out[at, :] = q
        scaled[at, :] = q * (1.0 / math.sqrt(HD))
        k_out[at, :] = turn(k_lin[at, :] + k_bias[...], at).astype(BF16)
        v_out[at, :] = (v_lin[at, :] + v_bias[...]).astype(BF16)

    lane = lax.broadcasted_iota(jnp.int32, (TILE, PAIR), 1)
    causal = lax.broadcasted_iota(jnp.int32, (TILE, TILE), 1) <= lax.broadcasted_iota(
        jnp.int32, (TILE, TILE), 0
    )
    for start in range(0, rows, TILE):
        at = pl.ds(start, TILE)
        first = first_ref[start // BLOCK]
        own = start // BLOCK * BLOCK
        outs = []
        for head in range(2):
            q = jnp.where(head_lanes(TILE, head), scaled[at, :], jnp.zeros((), BF16))
            parts = []
            for lower in range(0, own, BLOCK):
                s = mx(q, k_out[pl.ds(lower, BLOCK), :], NT)
                shut = jnp.where(first <= lower, 0.0, NEGATIVE).astype(F32)
                parts.append((s, lower, BLOCK, shut))
            if start > own:
                parts.append((mx(q, k_out[pl.ds(own, start - own), :], NT), own, start - own, None))
            s = jnp.where(causal, mx(q, k_out[at, :], NT), NEGATIVE)
            parts.append((s, start, TILE, None))
            peak = None
            for s, _, _, shut in parts:
                top = jnp.max(s, axis=-1, keepdims=True)
                if shut is not None:
                    top = top + shut
                peak = top if peak is None else jnp.maximum(peak, top)
            total = None
            acc = None
            for s, lower, size, shut in parts:
                base = peak if shut is None else peak - shut
                e = jnp.exp(s - base)
                add = jnp.sum(e, axis=-1, keepdims=True)
                total = add if total is None else total + add
                out = mx(e.astype(BF16), v_out[pl.ds(lower, size), :], NN)
                acc = out if acc is None else acc + out
            outs.append(acc / total)
            where_to = pair * 2 + head
            keep = log_out[at, :]
            if head == 0:
                keep = jnp.where(pair == 0, jnp.zeros_like(keep), keep)
            log_out[at, :] = jnp.where(lane == where_to, peak + jnp.log(total), keep)
        o_out[at, :] = jnp.where(lane < HD, outs[0], outs[1]).astype(BF16)


def attend(projected, bias_row, tables, firsts):
    rows, cols = projected.shape
    width_local = cols // 3
    pairs = width_local // PAIR

    def column(offset, rows_):
        return pl.BlockSpec((rows_, PAIR), lambda p: (0, p + offset * pairs))

    table = pl.BlockSpec((rows, PAIR), lambda p: (0, 0))
    area = rows * rows // 2 * width_local
    return pl.pallas_call(
        attend_kernel,
        grid=(pairs,),
        in_specs=[pl.BlockSpec(memory_space=pltpu.SMEM)]
        + [column(i, rows) for i in range(3)]
        + [column(i, 1) for i in range(3)]
        + [table] * 3,
        out_specs=[column(0, rows)] * 4 + [table],
        out_shape=[jax.ShapeDtypeStruct((rows, width_local), BF16)] * 4
        + [jax.ShapeDtypeStruct((rows, PAIR), F32)],
        scratch_shapes=[pltpu.VMEM((rows, PAIR), BF16)],
        cost_estimate=pl.CostEstimate(
            flops=4 * area, bytes_accessed=rows * cols * 8, transcendentals=area // HD
        ),
        name="attend",
    )(firsts, projected, projected, projected, bias_row, bias_row, bias_row, *tables)


def attend_back_kernel(
    first_ref,
    q_ref,
    k_ref,
    v_ref,
    o_ref,
    g_ref,
    log_ref,
    cos_ref,
    low_ref,
    high_ref,
    out_ref,
    sum_ref,
    k_acc,
    v_acc,
    k_turned,
    scaled,
):
    rows, _ = q_ref.shape
    pair = pl.program_id(0)
    pairs = out_ref.shape[1] // (3 * PAIR)
    half = ROT // 2
    factor = 1.0 / math.sqrt(HD)

    def turn_back(values, at):
        return (
            values * cos_ref[at, :]
            - pltpu.roll(values, PAIR - half, 1) * low_ref[at, :]
            - pltpu.roll(values, half, 1) * high_ref[at, :]
        )

    def put(which, at, values):
        lanes = pl.ds(pl.multiple_of((which * pairs + pair) * PAIR, PAIR), PAIR)
        low = values.astype(BF16)
        out_ref[at, lanes] = low
        return jnp.sum(low.astype(F32).reshape(TILE // 8, 8, PAIR), axis=0)

    def put_sum(which, values):
        lanes = pl.ds(pl.multiple_of((which * pairs + pair) * PAIR, PAIR), PAIR)
        sum_ref[:, lanes] = values

    k_acc[...] = jnp.zeros_like(k_acc)
    v_acc[...] = jnp.zeros_like(v_acc)
    k_turned[...] = k_ref[...].astype(F32).T.astype(BF16)
    scaled[...] = q_ref[...] * factor
    causal = lax.broadcasted_iota(jnp.int32, (TILE, TILE), 0) <= lax.broadcasted_iota(
        jnp.int32, (TILE, TILE), 1
    )
    lane = lax.broadcasted_iota(jnp.int32, (8, PAIR), 1)
    row = lax.broadcasted_iota(jnp.int32, (8, PAIR), 0)
    picks = jnp.where(lane // HD == row, 1.0, 0.0).astype(BF16)
    q_sum = jnp.zeros((8, PAIR), F32)
    for start in range(0, rows, TILE):
        at = pl.ds(start, TILE)
        first = first_ref[start // BLOCK]
        own = start // BLOCK * BLOCK
        product = g_ref[at, :].astype(F32) * o_ref[at, :].astype(F32)
        upper = product.astype(BF16)
        lower_part = (product - upper.astype(F32)).astype(BF16)
        deltas = mx(picks, upper, NT) + mx(picks, lower_part, NT)
        turned = []
        for head in range(2):
            mask = head_lanes(TILE, head)
            zero = jnp.zeros((), BF16)
            q = jnp.where(mask, scaled[at, :], zero)
            g = jnp.where(mask, g_ref[at, :], zero)
            log_row = log_ref[pl.ds(pair * 2 + head, 1), at]
            delta = deltas[head : head + 1, :]
            spans = [(lower, BLOCK, first <= lower) for lower in range(0, own, BLOCK)]
            if start > own:
                spans.append((own, start - own, None))
            spans.append((start, TILE, None))
            acc = None
            for lower, size, open_ in spans:
                keys = pl.ds(lower, size)
                s = mx(k_ref[keys, :], q, NT)
                base = log_row
                if open_ is not None:
                    base = log_row + jnp.where(open_, 0.0, -NEGATIVE).astype(F32)
                if lower == start:
                    s = jnp.where(causal, s, NEGATIVE)
                p = jnp.exp(s - base)
                v_acc[keys, :] += mx(p.astype(BF16), g, NN)
                dp = mx(v_ref[keys, :], g, NT)
                ds = (p * (dp - delta)).astype(BF16)
                k_acc[keys, :] += mx(ds, q, NN)
                part = mx(k_turned[pl.ds(head * HD, HD), keys], ds, NN)
                acc = part if acc is None else acc + part
            turned.append(acc)
        dq = jnp.concatenate(turned, axis=0).T * factor
        q_sum = q_sum + put(0, at, turn_back(dq, at))
    put_sum(0, q_sum)
    k_sum = jnp.zeros((8, PAIR), F32)
    v_sum = jnp.zeros((8, PAIR), F32)
    for start in range(0, rows, TILE):
        at = pl.ds(start, TILE)
        k_sum = k_sum + put(1, at, turn_back(k_acc[at, :], at))
        v_sum = v_sum + put(2, at, v_acc[at, :])
    put_sum(1, k_sum)
    put_sum(2, v_sum)


def attend_back(q, k, v, o, grads, log_rows, tables, firsts):
    rows, width_local = q.shape
    pairs = width_local // PAIR
    column = pl.BlockSpec((rows, PAIR), lambda p: (0, p))
    table = pl.BlockSpec((rows, PAIR), lambda p: (0, 0))
    area = rows * rows // 2 * width_local
    return pl.pallas_call(
        attend_back_kernel,
        grid=(pairs,),
        in_specs=[pl.BlockSpec(memory_space=pltpu.SMEM)]
        + [column] * 5
        + [pl.BlockSpec((PAIR, rows), lambda p: (0, 0))]
        + [table] * 3,
        out_specs=[
            pl.BlockSpec((rows, 3 * width_local), lambda p: (0, 0)),
            pl.BlockSpec((8, 3 * width_local), lambda p: (0, 0)),
        ],
        out_shape=[
            jax.ShapeDtypeStruct((rows, 3 * width_local), BF16),
            jax.ShapeDtypeStruct((8, 3 * width_local), F32),
        ],
        scratch_shapes=[
            pltpu.VMEM((rows, PAIR), F32),
            pltpu.VMEM((rows, PAIR), F32),
            pltpu.VMEM((PAIR, rows), BF16),
            pltpu.VMEM((rows, PAIR), BF16),
        ],
        cost_estimate=pl.CostEstimate(
            flops=10 * area, bytes_accessed=rows * width_local * 20, transcendentals=area // HD
        ),
        name="attend_back",
    )(firsts, q, k, v, o, grads, log_rows, *tables)


def rotary_tables(places, starts):
    lane = jnp.arange(PAIR, dtype=jnp.int32) % HD
    half = ROT // 2
    inverse = jnp.power(ROPE_BASE, -2.0 * (lane % half).astype(F32) / ROT)
    angles = (places - starts).astype(F32)[:, None] * inverse[None, :]
    cosine, sine = jnp.cos(angles), jnp.sin(angles)
    return (
        jnp.where(lane < ROT, cosine, 1.0),
        jnp.where(lane < half, -sine, 0.0),
        jnp.where((lane >= half) & (lane < ROT), sine, 0.0),
    )


def dot(a, b, dims=None):
    dims = dims or (((1,), (0,)), ((), ()))
    return lax.dot_general(a, b, dims, preferred_element_type=F32)


def gather(value, axis_name):
    return lax.all_gather(value, axis_name, axis=0, tiled=True)


def scatter(value, axis_name):
    return lax.psum_scatter(value, axis_name, scatter_dimension=0, tiled=True)


def mirror(value, axis_name, bit):
    size = lax.axis_size(axis_name)
    return lax.ppermute(value, axis_name, [(i, i ^ bit) for i in range(size)])


def small_gather(value, axis_name, late=None):
    bit = 1
    value = value[None]
    me = lax.axis_index(axis_name)
    while bit < lax.axis_size(axis_name):
        if late is not None and bit > 1:
            value = after(value, late)
        other = mirror(value, axis_name, bit)
        low = (me // bit) % 2 == 0
        value = jnp.concatenate(
            [jnp.where(low, value, other), jnp.where(low, other, value)], axis=0
        )
        bit *= 2
    return value


def small_scatter(value, axis_name):
    bit = lax.axis_size(axis_name) // 2
    me = lax.axis_index(axis_name)
    while bit:
        low = (me // bit) % 2 == 0
        first, second = jnp.split(value, 2, axis=0)
        value = jnp.where(low, first, second) + mirror(
            jnp.where(low, second, first), axis_name, bit
        )
        bit //= 2
    return value[0]


def shift(value, axis_name, pairs):
    return lax.ppermute(value, axis_name, pairs)


def after(value, *needed):
    return lax.optimization_barrier((value,) + needed)[0]


def ring(axis_name):
    n = lax.axis_size(axis_name)
    return [(i, (i + 1) % n) for i in range(n)]


class Order:
    def __init__(self, token):
        self.token = token

    def pin(self, *values):
        out = lax.optimization_barrier(values + (self.token,))[:-1]
        self.token = out[0]
        return out if len(out) > 1 else out[0]

    def done(self, value):
        self.token = value
        return value


class Gather:
    def __init__(self, order, value):
        self.order, self.step = order, 0
        self.n = lax.axis_size("tensor")
        self.own = value
        self.right, self.left = [value], [value]

    def hop(self):
        self.step += 1
        n, step = self.n, self.step
        right, left = self.order.pin(self.right[-1], self.left[-1])
        self.right.append(shift(right, "tensor", [(i, i + 1) for i in range(step - 1, n - 1)]))
        self.left.append(shift(left, "tensor", [(i, i - 1) for i in range(1, n - step + 1)]))

    def slots(self):
        me = lax.axis_index("tensor")
        return [self.own] + [
            jnp.where(me >= s, self.right[s], self.left[self.n - s]) for s in range(1, self.n)
        ]


class Scatter:
    def __init__(self, order, pieces):
        self.order, self.step = order, 0
        self.n = lax.axis_size("tensor")
        self.pieces = pieces
        self.right = self.left = None

    def hop(self):
        self.step += 1
        n, step = self.n, self.step
        right, left = self.pieces[n - step], self.pieces[step]
        if step > 1:
            right = (right.astype(F32) + self.right.astype(F32)).astype(BF16)
            left = (left.astype(F32) + self.left.astype(F32)).astype(BF16)
        right, left = self.order.pin(right, left)
        self.right = shift(right, "tensor", [(i, i + 1) for i in range(min(step, n - 1))])
        self.left = shift(left, "tensor", [(i, i - 1) for i in range(max(n - step, 1), n)])

    def total(self):
        return self.pieces[0].astype(F32) + self.right.astype(F32) + self.left.astype(F32)


def place(slots, axis_name):
    n = len(slots)
    me = lax.axis_index(axis_name)
    rows = slots[0].shape[0]
    out = jnp.zeros((n * rows,) + slots[0].shape[1:], slots[0].dtype)
    for s, slot in enumerate(slots):
        out = lax.dynamic_update_slice_in_dim(out, slot, lax.rem(me - s + n, n) * rows, 0)
    return out


def row_piece(value, k, rows, axis_name):
    n = lax.axis_size(axis_name)
    me = lax.axis_index(axis_name)
    return lax.dynamic_slice_in_dim(value, lax.rem(me + k, n) * rows, rows, 0)


def per_device(
    activations,
    sequence_start,
    norm_gain,
    norm_bias,
    projection,
    biases,
    rotary_bias,
    merge_weight,
    expand_weight,
    down_weight,
    cotangent,
):
    n_dp = lax.axis_size("dp")
    n_tensor = lax.axis_size("tensor")
    tok_rows, width = activations.shape
    group_rows = tok_rows * n_tensor
    factor = 1.0 / math.sqrt(HD)
    heads_local = biases.shape[1]
    width_local = heads_local * HD
    hidden_local = down_weight.shape[0]

    units = [activations]
    for step in range(1, n_tensor):
        units.append(shift(units[-1], "tensor", ring("tensor")))

    norm_part = width // (n_dp * n_tensor)
    packed = jnp.concatenate(
        [
            jnp.concatenate([norm_gain, norm_bias], axis=0).reshape(-1),
            sequence_start.astype(BF16),
        ]
    )
    packed = small_gather(packed, "tensor")
    starts = packed[:, 4 * norm_part :].reshape(group_rows).astype(jnp.int32)
    second = jnp.concatenate(
        [
            packed[:, : 4 * norm_part].reshape(-1),
            biases.reshape(-1),
            rotary_bias.reshape(-1),
        ]
    )
    second = small_gather(second, "dp", units[min(2, n_tensor - 1)])
    cut = n_tensor * 4 * norm_part
    norms = second[:, :cut].reshape(n_dp, n_tensor, 4, norm_part)
    norms = norms.transpose(2, 0, 1, 3).reshape(4, width).astype(F32)
    gains_all, shifts_all = norms[:2], norms[2:]
    cut_two = cut + biases.size
    bias_float = second[:, cut:cut_two].reshape(n_dp, 2, heads_local, HD // n_dp)
    bias_float = bias_float.transpose(1, 2, 0, 3).reshape(2, heads_local, HD).astype(F32)
    rotary_full = second[:, cut_two:].reshape(n_dp, heads_local, ROT // n_dp)
    rotary_full = rotary_full.transpose(1, 0, 2).reshape(heads_local, ROT).astype(F32)

    chunk_rows = tok_rows // CHUNKS

    def split(value):
        return [value[c * chunk_rows : (c + 1) * chunk_rows] for c in range(CHUNKS)]

    def whole(slots_by_chunk):
        slots = [jnp.concatenate(pieces, axis=0) for pieces in zip(*slots_by_chunk)]
        return place(slots, "tensor")

    project_full = gather(projection.reshape(-1, 3 * width_local), "dp")
    merge_full = gather(merge_weight.T, "dp")
    expand_full = gather(expand_weight.reshape(-1, 2 * hidden_local), "dp")
    down_full = gather(down_weight.T, "dp")
    inputs_float = activations.astype(F32)
    places = jnp.arange(group_rows, dtype=jnp.int32)
    tables = rotary_tables(places, starts)
    firsts = starts[::BLOCK]
    bias_row = jnp.concatenate(
        [
            bias_float[0].reshape(-1),
            jnp.pad(rotary_full, ((0, 0), (0, HD - ROT))).reshape(-1),
            bias_float[1].reshape(-1),
        ]
    )[None]
    me = lax.axis_index("tensor")
    normed_all = jnp.zeros((group_rows, width), BF16)
    projected = jnp.zeros((group_rows, 3 * width_local), F32)
    for step in range(n_tensor):
        if step > 1:
            units[step] = after(units[step], projected)
        unit, _ = norm_stats(units[step].astype(F32))
        normed = (unit * gains_all[0] + shifts_all[0]).astype(BF16)
        to = lax.rem(me - step + n_tensor, n_tensor) * tok_rows
        normed_all = lax.dynamic_update_slice_in_dim(normed_all, normed, to, 0)
        projected = lax.dynamic_update_slice_in_dim(projected, dot(normed, project_full), to, 0)
    order = Order(projected)
    last = n_tensor - 1

    cot_gather = Gather(order, cotangent)
    cot_gather.hop()
    queries, keys_all, values, attended_flat, logs = attend(
        order.pin(projected), bias_row, tables, firsts
    )
    order.done(attended_flat)

    def pieces_of(value, k):
        rows = row_piece(order.pin(value), k, tok_rows, "tensor")
        return order.done(dot(rows, merge_full, COLS).astype(BF16))

    merged = [None] * n_tensor
    for k in (last, 1):
        if merged[k] is None:
            merged[k] = pieces_of(attended_flat, k)

    def part(c):
        return slice(c * chunk_rows, (c + 1) * chunk_rows)

    class Late:
        def __init__(self, c):
            self.c = c

        def __getitem__(self, k):
            if merged[k] is None:
                merged[k] = pieces_of(attended_flat, k)
            return merged[k][part(self.c)]

    streams = [Scatter(order, Late(c)) for c in range(CHUNKS)]
    for step in range(1, n_tensor):
        for c in range(CHUNKS):
            streams[c].hop()
            if c == 0 and step < last:
                merged_next = Late(c)[n_tensor - step - 1]
                if step == 1:
                    merged_next = Late(c)[0]
        if step > 1 or n_tensor == 2:
            if cot_gather.step < last:
                cot_gather.hop()
    while cot_gather.step < last:
        cot_gather.hop()

    x_chunks = split(inputs_float)
    residuals, units_two, scales_two, gathers = [], [], [], []
    for c in range(CHUNKS):
        residual = order.done(x_chunks[c] + streams[c].total())
        unit_two, scale_two = norm_stats(residual)
        normed_two = (unit_two * gains_all[1] + shifts_all[1]).astype(BF16)
        residuals.append(residual)
        gathers.append(Gather(order, normed_two))
        gathers[c].hop()
    cot_slots = cot_gather.slots()
    hidden_grads = [None] * CHUNKS
    cot_chunks = [None] * CHUNKS
    for step in range(2, n_tensor):
        for c in range(CHUNKS):
            gathers[c].hop()
            if step == 2:
                cot_chunks[c] = place([slot[part(c)] for slot in cot_slots], "tensor")
                hidden_grads[c] = order.done(dot(order.pin(cot_chunks[c]), down_full))

    def feed(c):
        normed_two_all = order.pin(place(gathers[c].slots(), "tensor"))
        gate = dot(normed_two_all, expand_full[:, :hidden_local])
        up = dot(normed_two_all, expand_full[:, hidden_local:])
        sig = 1.0 / (1.0 + jnp.exp(-gate))
        silu = gate * sig
        hidden = (silu * up).astype(BF16)
        gate_grad = (hidden_grads[c] * up * sig * (1.0 + gate * (1.0 - sig))).astype(BF16)
        up_grad = (hidden_grads[c] * silu).astype(BF16)
        expand_grads = order.done(jnp.concatenate([gate_grad, up_grad], axis=1))
        return normed_two_all, hidden, expand_grads

    def feed_back(expand_grads):
        back = order.done(dot(order.pin(expand_grads), expand_full, COLS).astype(BF16))
        return Scatter(order, [row_piece(back, k, chunk_rows, "tensor") for k in range(n_tensor)])

    fed_parts, streams = [], []
    for c in range(CHUNKS):
        fed_parts.append(feed(c))
        if c:
            streams[c - 1].hop()
        streams.append(feed_back(fed_parts[c][2]))
        streams[c].hop()
    normed_two_all, hidden, expand_grads = (
        jnp.concatenate([piece[i] for piece in fed_parts], axis=0) for i in range(3)
    )
    out_grad_all = jnp.concatenate(cot_chunks, axis=0)

    def norm_two_back(c):
        normed_two_grad = order.done(streams[c].total())
        unit_two, scale_two = norm_stats(residuals[c])
        residual_grad = cotangent[part(c)].astype(F32) + norm_back(
            unit_two, scale_two, gains_all[1], normed_two_grad
        )
        sums = (jnp.sum(normed_two_grad * unit_two, axis=0), jnp.sum(normed_two_grad, axis=0))
        gather_ = Gather(order, residual_grad.astype(BF16))
        gather_.hop()
        return residual_grad, sums, gather_

    while streams[0].step < last:
        streams[0].hop()
        if streams[1].step < last - 1:
            streams[1].hop()
    down_part = order.done(dot(order.pin(out_grad_all), hidden, ROWS).astype(BF16))
    while streams[1].step < last - 1:
        streams[1].hop()
    backs = [norm_two_back(0)]
    while streams[1].step < last:
        streams[1].hop()
    expand_part = order.done(dot(order.pin(normed_two_all), expand_grads, ROWS).astype(BF16))
    backs.append(norm_two_back(1))
    residual_grad = jnp.concatenate([back[0] for back in backs], axis=0)
    gain_two = sum(back[1][0] for back in backs)
    shift_two = sum(back[1][1] for back in backs)
    down_grad = scatter(down_part, "dp").astype(F32).T
    expand_grad = scatter(expand_part, "dp").astype(F32)
    expand_grad = expand_grad.reshape(-1, 2, hidden_local)

    fed = []
    for c in range(CHUNKS):
        rows = hidden[c * n_tensor * chunk_rows : (c + 1) * n_tensor * chunk_rows]
        fed.append(order.done(dot(order.pin(rows), down_full, COLS).astype(BF16)))
    fed = [
        jnp.concatenate([row_piece(value, k, chunk_rows, "tensor") for value in fed], axis=0)
        for k in range(n_tensor)
    ]
    fed_scatter = Scatter(order, fed)
    for step in range(2, n_tensor):
        for c in range(CHUNKS):
            backs[c][2].hop()
        fed_scatter.hop()
    branch_slots = [
        jnp.concatenate(pieces, axis=0) for pieces in zip(*[back[2].slots() for back in backs])
    ]
    branch_all = order.done(place(branch_slots, "tensor"))
    attended_grad = order.done(dot(branch_all, merge_full).astype(BF16))
    merge_part = order.done(dot(order.pin(branch_all), attended_flat, ROWS).astype(BF16))
    fed_scatter.hop()
    layer_output = (jnp.concatenate(residuals, axis=0) + fed_scatter.total()).astype(BF16)
    merge_grad = scatter(merge_part, "dp").astype(F32).T
    project_grads, project_sums = attend_back(
        queries,
        keys_all,
        values,
        attended_flat,
        after(order.pin(attended_grad), down_grad),
        logs.T,
        tables,
        firsts,
    )
    order.done(project_grads)
    normed_parts, sent = [None] * n_tensor, None
    gain_one, shift_one = 0.0, 0.0
    for step in range(1, n_tensor + 1):
        k = n_tensor - step
        rows = row_piece(order.pin(project_grads), k, tok_rows, "tensor")
        piece = order.done(dot(rows, project_full, COLS))
        unit, _ = norm_stats(units[(n_tensor - k) % n_tensor].astype(F32))
        gain_one = gain_one + jnp.sum(piece * unit, axis=0)
        shift_one = shift_one + jnp.sum(piece, axis=0)
        if sent is not None:
            piece = piece.astype(BF16).astype(F32) + sent.astype(F32)
        if k == 1:
            piece = after(piece, expand_grad, layer_output)
        if k:
            sent = shift(order.pin(piece.astype(BF16)), "tensor", ring("tensor"))
        if step == 1:
            project_part = dot(order.pin(normed_all), project_grads, ROWS).astype(BF16)
            order.done(project_part)
    normed_grad = piece
    projection_grad = scatter(project_part, "dp").astype(F32)
    projection_grad = projection_grad.reshape(-1, 3, width_local)

    norm_sums = jnp.stack(
        [
            gain_one,
            gain_two,
            shift_one,
            shift_two,
        ]
    )
    norm_sums = norm_sums.reshape(4, n_dp, n_tensor, norm_part).transpose(2, 1, 0, 3)
    norm_sums = small_scatter(norm_sums.reshape(n_tensor, -1), "tensor").reshape(n_dp, 4 * norm_part)
    project_sums = jnp.sum(project_sums, axis=0).reshape(3, heads_local, HD)
    bias_sums = project_sums[::2].reshape(2, heads_local, n_dp, HD // n_dp).transpose(2, 0, 1, 3)
    rotary_sums = project_sums[1, :, :ROT]
    rotary_sums = rotary_sums.reshape(heads_local, n_dp, ROT // n_dp).transpose(1, 0, 2)
    small = jnp.concatenate(
        [norm_sums, bias_sums.reshape(n_dp, -1), rotary_sums.reshape(n_dp, -1)], axis=1
    )
    small = small_scatter(small, "dp").reshape(-1)
    norm_sums = small[: 4 * norm_part].reshape(2, 2, norm_part)
    cut = 4 * norm_part + 2 * heads_local * (HD // n_dp)
    biases_grad = small[4 * norm_part : cut].reshape(2, heads_local, HD // n_dp)
    rotary_grad = small[cut:].reshape(heads_local, ROT // n_dp)
    normed_grad = after(normed_grad, merge_grad, norm_sums, biases_grad)
    unit_one, scale_one = norm_stats(inputs_float)
    input_grad = residual_grad + norm_back(unit_one, scale_one, gains_all[0], normed_grad)
    return (
        layer_output,
        input_grad,
        norm_sums[0],
        norm_sums[1],
        projection_grad,
        biases_grad,
        rotary_grad,
        merge_grad,
        expand_grad,
        down_grad,
    )


def solution(mesh):
    return jax.shard_map(
        per_device,
        mesh=mesh,
        in_specs=(
            P(("dp", "tensor"), None),
            P(("dp", "tensor")),
            P(None, ("dp", "tensor")),
            P(None, ("dp", "tensor")),
            P("dp", None, "tensor"),
            P(None, "tensor", "dp"),
            P("tensor", "dp"),
            P("tensor", "dp"),
            P("dp", None, "tensor"),
            P("tensor", "dp"),
            P(("dp", "tensor"), None),
        ),
        out_specs=(
            P(("dp", "tensor"), None),
            P(("dp", "tensor"), None),
            P(None, ("dp", "tensor")),
            P(None, ("dp", "tensor")),
            P("dp", None, "tensor"),
            P(None, "tensor", "dp"),
            P("tensor", "dp"),
            P("tensor", "dp"),
            P("dp", None, "tensor"),
            P("tensor", "dp"),
        ),
        check_vma=False,
    )
```
